32 devices in a mesh: wide: 8 (over y, x, core), narrow: 4 (over z).
Axes of the slice: x: 2, y: 2, z: 4, core: 2. Of those that a mesh axis runs over, the one named last changes fastest.
Arguments:
- tokens: bfloat16 [8192, 1120], P('wide', 'narrow'), may hold values from -6 to 6
- lengths: int32 [8], P('wide'), may hold values from 1 to 1024, 5120 in all
- qkv_weight: bfloat16 [1120, 3, 1120], P(None, None, 'narrow'), may hold values from -0.1875 to 0.1875
- qv_bias: float32 [2, 1120], P(None, 'narrow'), may hold values from -3 to 3
- out_weight: bfloat16 [1120, 1120], P('narrow'), may hold values from -1.5 to 1.5
- out_bias: float32 [1120], replicated, may hold values from -3 to 3
- gain_one: float32 [1120], replicated, may hold values from 0.1 to 1.9
- shift_one: float32 [1120], replicated, may hold values from -2 to 2
- gain_two: float32 [1120], replicated, may hold values from 0.1 to 1.9
- shift_two: float32 [1120], replicated, may hold values from -2 to 2
- up_weight: bfloat16 [1120, 4480], P(None, 'narrow'), may hold values from -0.1875 to 0.1875
- up_bias: float32 [4480], P('narrow'), may hold values from -3 to 3
- down_weight: bfloat16 [4480, 1120], P('narrow'), may hold values from -0.09375 to 0.09375
- down_bias: float32 [1120], replicated, may hold values from -3 to 3
- cotangent: bfloat16 [8192, 1120], P('wide', 'narrow'), may hold values from -6 to 6
Outputs:
- output: bfloat16 [8192, 1120], P('wide', 'narrow')
- grad_tokens: bfloat16 [8192, 1120], P('wide', 'narrow')
- grad_qkv_weight: float32 [1120, 3, 1120], P(None, None, 'narrow')
- grad_qv_bias: float32 [2, 1120], P(None, 'narrow')
- grad_out_weight: float32 [1120, 1120], P('narrow')
- grad_out_bias: float32 [1120], P('narrow')
- grad_gain_one: float32 [1120], P('narrow')
- grad_shift_one: float32 [1120], P('narrow')
- grad_gain_two: float32 [1120], P('narrow')
- grad_shift_two: float32 [1120], P('narrow')
- grad_up_weight: float32 [1120, 4480], P(None, 'narrow')
- grad_up_bias: float32 [4480], P('narrow')
- grad_down_weight: float32 [4480, 1120], P('narrow')
- grad_down_bias: float32 [1120], P('narrow')
The draws below stay inside these ranges and needn't reach their ends.
Inputs may be any that keep to these rules, and one draw needn't show every extreme that they name: `lengths`: valid tokens of each cell, counted from its first slot; the longest cell is full, and all cells together hold 5120 valid tokens.
All inputs are finite; a program needn't handle non-finite values. No bound on the sum of `lengths` on one device may be relied on, other than what follows from the above.
Results may differ from the reference program's by a relative error of at most 0.017.
Values may be sent and summed in bfloat16 or wider, within the bound.
No kernel may reach another device: no remote copies, remote signals or barrier semaphores. Data moves between devices by JAX's collectives and lax.ppermute only.
A program may use at most 192 MiB of HBM per device.

```python
import math
import jax
import jax.numpy as jnp
import numpy as np
from jax import lax

D = 1120
HEADS = 20
HD = 56
FF = 4480
SEQ = 1024
CELLS = 8
TOKENS = 8192


def block_levels(own_key, dims, cuts, low, high):
    loudness, own = 1.0, jax.random.fold_in(own_key, 6)
    for position, parts in cuts:
        draws = jnp.exp(jax.random.uniform(jax.random.fold_in(own, position), (parts,), jnp.float32, low / len(cuts), high / len(cuts)))
        loudness = loudness * jnp.repeat(draws, dims[position] // parts).reshape([-1 if axis == position else 1 for axis in range(len(dims))])
    return loudness


def profile(amount, total, most, skew):
    portions = [(1 << 20) // math.isqrt(standing ** skew) + 1 for standing in range(2, amount + 1)]
    spare, given = total - most - (amount - 1), [1] * (amount - 1)
    while spare > 0:
        candidates = [i for i in range(amount - 1) if given[i] < most]
        pool, left = sum([portions[i] for i in candidates]), spare
        for i in candidates:
            extra = min(most - given[i], max(1, left * portions[i] // pool), spare)
            given[i] = given[i] + extra
            spare = spare - extra
    return np.array([most] + given)


def uneven_parts(own_key, number_of, total, reach, slope):
    if number_of == 2:
        one = jax.random.randint(own_key, (), max(1, total - reach), min(reach, total - 1) + 1)
        return jnp.stack([one, total - one])
    sizes = jnp.asarray(profile(number_of, total, reach, slope), jnp.int32)
    pairs = (number_of - 1) // 2
    giver, sink = sizes[1:1 + 2 * pairs:2], sizes[2:2 + 2 * pairs:2]
    slack = jnp.minimum(giver - 1, reach - sink)
    shifted = jax.random.randint(jax.random.fold_in(own_key, 1), (pairs,), 0, 1 << 20) % (slack + 1)
    sizes = sizes.at[1:1 + 2 * pairs:2].set(giver - shifted).at[2:2 + 2 * pairs:2].set(sink + shifted)
    return sizes[jax.random.permutation(jax.random.fold_in(own_key, 2), number_of)]


def gaussian(stream_key, dims, deviation, bound, split=(), held_as=jnp.bfloat16):
    entries = deviation * jax.random.normal(stream_key, dims, jnp.float32)
    if split:
        entries = entries * block_levels(stream_key, dims, split, -0.22, 0.18)
    return jnp.clip(entries, -bound, bound).astype(held_as)


def setup_inputs(seed: int = 0) -> dict:
    streams_of = jax.random.split(jax.random.key(seed), 16)
    return {
        "tokens": gaussian(streams_of[0], (TOKENS, D), 1.0, 6.0, ((0, 8), (1, 4))),
        "lengths": uneven_parts(streams_of[1], CELLS, CELLS * SEQ * 5 // 8, SEQ, 1).astype(jnp.int32),
        "qkv_weight": gaussian(streams_of[2], (D, 3, D), D ** -0.5, 0.1875, ((2, 4),)),
        "qv_bias": gaussian(streams_of[3], (2, D), 0.5, 3.0, ((1, 4),), jnp.float32),
        "out_weight": gaussian(streams_of[4], (D, D), (max(D * 16 // SEQ, 1)) ** -0.5, 1.5, ((0, 4),)),
        "out_bias": gaussian(streams_of[5], (D,), 0.5, 3.0, (), jnp.float32),
        "gain_one": jnp.clip(1.0 + 0.18 * jax.random.normal(streams_of[6], (D,), jnp.float32), 0.1, 1.9),
        "shift_one": gaussian(streams_of[7], (D,), 0.3, 2.0, (), jnp.float32),
        "gain_two": jnp.clip(1.0 + 0.18 * jax.random.normal(streams_of[8], (D,), jnp.float32), 0.1, 1.9),
        "shift_two": gaussian(streams_of[9], (D,), 0.3, 2.0, (), jnp.float32),
        "up_weight": gaussian(streams_of[10], (D, FF), D ** -0.5, 0.1875, ((1, 4),)),
        "up_bias": gaussian(streams_of[11], (FF,), 0.5, 3.0, ((0, 4),), jnp.float32),
        "down_weight": gaussian(streams_of[12], (FF, D), FF ** -0.5, 0.09375, ((0, 4),)),
        "down_bias": gaussian(streams_of[13], (D,), 0.5, 3.0, (), jnp.float32),
        "cotangent": gaussian(streams_of[14], (TOKENS, D), 1.0, 6.0, ((0, 8), (1, 4))),
    }


@jax.custom_vjp
def low(v):
    return lax.optimization_barrier(v.astype(jnp.bfloat16)).astype(jnp.float32)

@jax.custom_vjp
def low_back(v):
    return v

def low_keep(v):
    return (low(v), None)

def low_pass(kept, grad):
    return (grad,)

def back_keep(v):
    return (v, None)

def back_low(kept, grad):
    return (low(grad),)
low.defvjp(low_keep, low_pass)
low_back.defvjp(back_keep, back_low)
NORM_EPS = 1e-05
PRECISE = lax.Precision.HIGHEST

def norm_rows(values, gain, shift):
    row_mean = lax.optimization_barrier(jnp.mean(values, axis=-1, keepdims=True))
    centered = values - row_mean
    variance = lax.optimization_barrier(jnp.mean(centered * centered, axis=-1, keepdims=True))
    return centered * lax.rsqrt(variance + NORM_EPS) * gain + shift

def product(left, right):
    return jnp.dot(left, right, precision=PRECISE, preferred_element_type=jnp.float32)

def block_forward(weights, cell_rows, length):
    qkv_weight, qv_bias, out_weight, out_bias, gain_one, shift_one, gain_two, shift_two, up_weight, up_bias, down_weight, down_bias = weights
    seq_len = cell_rows.shape[0]
    normed = low(norm_rows(cell_rows, gain_one, shift_one))
    projected = product(normed, qkv_weight.reshape(D, 3 * D)).reshape(seq_len, 3, HEADS, HD)
    queries = low_back(low(projected[:, 0] + qv_bias[0].reshape(HEADS, HD)))
    key_rows = low_back(low(projected[:, 1]))
    values = low_back(low(projected[:, 2] + qv_bias[1].reshape(HEADS, HD)))
    scores = low_back(jnp.einsum('qhd,khd->hqk', queries, key_rows, precision=PRECISE) * HD ** (-0.5))
    row_ids = jnp.arange(seq_len)[:, None]
    col_ids = jnp.arange(seq_len)[None, :]
    allowed = (col_ids <= row_ids) & (col_ids < length)
    scores = jnp.where(allowed[None], scores, -1e+30)
    attend = low(jax.nn.softmax(scores, axis=-1))
    attended = jnp.einsum('hqk,khd->qhd', attend, values, precision=PRECISE).reshape(seq_len, D)
    attended = low_back(low(attended))
    residual = cell_rows + low_back(product(attended, out_weight)) + out_bias
    normed_two = low(norm_rows(residual, gain_two, shift_two))
    pre_gelu = low_back(product(normed_two, up_weight) + up_bias)
    active = low(jax.nn.gelu(pre_gelu, approximate=True))
    return residual + product(active, down_weight) + down_bias

def reference(tokens, lengths, qkv_weight, qv_bias, out_weight, out_bias, gain_one, shift_one, gain_two, shift_two, up_weight, up_bias, down_weight, down_bias, cotangent):
    params = tuple((item.astype(jnp.float32) for item in (qkv_weight, qv_bias, out_weight, out_bias, gain_one, shift_one, gain_two, shift_two, up_weight, up_bias, down_weight, down_bias)))
    cells = tokens.astype(jnp.float32).reshape(CELLS, SEQ, D)
    grads_in = cotangent.astype(jnp.float32).reshape(CELLS, SEQ, D)

    def per_cell(carried, item):
        cell_rows, cell_grad, length = item
        out_rows, pull = jax.vjp(lambda weights, rows: block_forward(weights, rows, length), params, cell_rows)
        weight_grads, row_grads = pull(cell_grad)
        carried = jax.tree.map(lambda left, right: left + right, carried, weight_grads)
        return (carried, (out_rows.astype(jnp.bfloat16), row_grads.astype(jnp.bfloat16)))
    empty_grads = jax.tree.map(jnp.zeros_like, params)
    summed, (outputs, row_grads) = lax.scan(per_cell, empty_grads, (cells, grads_in, lengths))
    return (outputs.reshape(TOKENS, D), row_grads.reshape(TOKENS, D), summed[0], summed[1], summed[2], summed[3], summed[4], summed[5], summed[6], summed[7], summed[8], summed[9], summed[10], summed[11])
```

```python
import itertools

import jax
import jax.numpy as jnp
from jax import lax
from jax.sharding import Mesh, PartitionSpec as P

HD = 56
NORM_EPS = 1e-05
AXES = ("hi", "b1", "b0", "core", "zh", "zl")
BF = jnp.bfloat16
F32 = jnp.float32


def mm(left, right, dims):
    return lax.dot_general(left, right, (dims, ((), ())), preferred_element_type=F32)


def route(high, target):
    pairs = []
    sizes = (high, 2, 2, 2, 2, 2)

    def flat(place):
        index = 0
        for size, value in zip(sizes, place):
            index = index * size + value
        return index

    for place in itertools.product(*[range(size) for size in sizes]):
        goal = target(*place)
        if goal is not None:
            pairs.append((flat(place), flat(goal)))
    return pairs


def half_rows(rows):
    return -(-(rows // 8) // 2) * 8


def pick(bit, first, second):
    return jnp.where(bit == 0, first, second)


def split(array, bit):
    rows = array.shape[0]
    size = half_rows(rows)
    low, top = array[:size], array[rows - size :]
    return pick(bit, low, top), pick(bit, top, low)


def merge(own, other, bit, rows):
    size = own.shape[0]
    first = jnp.concatenate([own[: rows - size], other], axis=0)
    second = jnp.concatenate([other[: rows - size], own], axis=0)
    return pick(bit, first, second)


def norm_parts(values):
    row_mean = jnp.mean(values, axis=0, keepdims=True)
    centered = values - row_mean
    variance = jnp.mean(centered * centered, axis=0, keepdims=True)
    inv_std = lax.rsqrt(variance + NORM_EPS)
    return row_mean, inv_std


def build(high):
    def all_places(fn):
        return route(high, fn)

    swap_core = all_places(lambda h, p, q, c, a, b: (h, p, q, 1 - c, a, b))
    swap_low = all_places(lambda h, p, q, c, a, b: (h, p, q, c, a, 1 - b))
    swap_high = all_places(lambda h, p, q, c, a, b: (h, p, q, c, 1 - a, b))
    swap_b0 = all_places(lambda h, p, q, c, a, b: (h, p, 1 - q, c, a, b))
    swap_b1 = all_places(lambda h, p, q, c, a, b: (h, 1 - p, q, c, a, b))
    regroup = all_places(lambda h, p, q, c, a, b: (h, p, q, a, c, b))
    parts_b0 = all_places(lambda h, p, q, c, a, b: (h, p, 1 - q, c, a, b) if c != a else (h, p, q, c, a, b))
    parts_b1 = all_places(lambda h, p, q, c, a, b: (h, 1 - p, q, c, a, b) if c != a else (h, p, q, c, a, b))
    home_send = all_places(lambda h, p, q, c, a, b: (h, p, q, c, c, b) if c != a else None)
    home_b0 = all_places(lambda h, p, q, c, a, b: (h, p, 1 - q, c, a, b) if c == a else None)
    home_b1 = all_places(lambda h, p, q, c, a, b: (h, 1 - p, q, c, a, b) if c == a else None)
    home_core = all_places(lambda h, p, q, c, a, b: (h, p, q, 1 - c, a, b) if c == a else None)

    def send(value, pairs):
        return lax.ppermute(value, AXES, pairs)

    def per_device(
        tokens,
        lengths,
        qkv_weight,
        qv_bias,
        out_weight,
        out_bias,
        gain_one,
        shift_one,
        gain_two,
        shift_two,
        up_weight,
        up_bias,
        down_weight,
        down_bias,
        cotangent,
    ):
        core = lax.axis_index("core")
        zh = lax.axis_index("zh")
        zl = lax.axis_index("zl")
        b0 = lax.axis_index("b0")
        b1 = lax.axis_index("b1")
        home = core == zh
        part = 2 * b1 + b0
        shard = 2 * core + zl

        seq_len, share = tokens.shape
        model = qkv_weight.shape[0]
        local_cols = qkv_weight.shape[2]
        head_count = local_cols // HD
        score_scale = HD ** (-0.5)

        def gather4(own):
            other = send(own, swap_low)
            half = merge(own, other, zl, 2 * share)
            other_half = send(half, swap_core)
            return merge(half, other_half, core, 4 * share)

        def scatter4(partial):
            keep, away = split(partial, core)
            keep = keep + send(away.astype(BF), swap_core).astype(F32)
            mine, away = split(keep, zl)
            return mine + send(away.astype(BF), swap_low).astype(F32)

        def sums4(partial):
            partial = partial + send(partial, swap_core)
            return partial + send(partial, swap_low)

        def own_slice(vector):
            return lax.dynamic_slice_in_dim(vector, shard * share, share, 0)[:, None]

        tokens_own = send(tokens.T, regroup)
        other_length = send(lengths, swap_core)
        length = jnp.where(home, lengths, other_length)[0]

        def gather_parts(weights, sizes, steps):
            def piece(index):
                pieces = [
                    lax.dynamic_slice_in_dim(weight, step * index, size, 0)
                    for weight, size, step in zip(weights, sizes, steps)
                ]
                return pieces[0] if len(pieces) == 1 else jnp.concatenate(pieces, axis=0)

            got = [send(piece(part), regroup)]
            got.append(send(jnp.where(home, piece(part ^ 1), got[0]), parts_b0))
            got.append(send(jnp.where(home, piece(part ^ 2), got[0]), parts_b1))
            total = sum(sizes)
            cut = half_rows(total)
            last = piece(part ^ 3)
            top = send(jnp.where(home, last[:cut], got[2][:cut]), parts_b0)
            bottom = send(jnp.where(home, last[cut:], got[1][cut:]), parts_b1)
            got.append(jnp.concatenate([top, bottom], axis=0))
            results = []
            start = 0
            for weight, size, step in zip(weights, sizes, steps):
                full = jnp.zeros_like(weight)
                for k in range(4):
                    full = lax.dynamic_update_slice_in_dim(
                        full, got[k][start : start + size], (part ^ k) * step, 0
                    )
                results.append(full)
                start += size
            return results

        qkv_flat = qkv_weight.transpose(1, 2, 0).reshape(3 * local_cols, model)

        def steps_of(rows):
            step = (rows // 4) // 8 * 8
            return rows - 3 * step, step

        def gathered(weights):
            sizes, steps = zip(*[steps_of(weight.shape[0]) for weight in weights])
            return gather_parts(weights, sizes, steps)

        qkv_t, out_w = gathered([qkv_flat, out_weight])
        biases = send(jnp.concatenate([qv_bias.reshape(-1), up_bias]), regroup)
        query_bias = biases[:local_cols, None]
        value_bias = biases[local_cols : 2 * local_cols, None]
        up_b = biases[2 * local_cols :, None]
        full_cell = gather4(tokens_own).astype(F32)
        cot_own = send(cotangent.T, regroup)
        up_w, down_w = gathered([up_weight, down_weight])
        cot = gather4(cot_own)

        mean_one, inv_one = norm_parts(full_cell)
        unit_one = (full_cell - mean_one) * inv_one
        normed_low = (unit_one * gain_one[:, None] + shift_one[:, None]).astype(BF)
        projected = mm(qkv_t, normed_low, ((1,), (0,)))
        queries = (projected[:local_cols] + query_bias).astype(BF).reshape(head_count, HD, seq_len)
        keys = projected[local_cols : 2 * local_cols].astype(BF).reshape(head_count, HD, seq_len)
        values = (projected[2 * local_cols :] + value_bias).astype(BF).reshape(head_count, HD, seq_len)

        block_rows = min(512, seq_len)
        block_count = seq_len // block_rows

        def allowed_block(start, stop):
            key_ids = jnp.arange(stop)[:, None]
            row_ids = start + jnp.arange(block_rows)[None, :]
            return ((key_ids <= row_ids) & (key_ids < length))[None]

        def scores_of(start, stop):
            scores = (
                jnp.einsum(
                    "hdk,hdq->hkq",
                    keys[:, :, :stop],
                    queries[:, :, start:stop],
                    preferred_element_type=F32,
                )
                * score_scale
            )
            return jnp.where(allowed_block(start, stop), scores, -1e30)

        attended_parts = []
        log_totals = []
        for block in range(block_count):
            start, stop = block * block_rows, (block + 1) * block_rows
            scores = scores_of(start, stop)
            peak = jnp.max(scores, axis=1, keepdims=True)
            lifted = jnp.exp(scores - peak)
            total = jnp.sum(lifted, axis=1, keepdims=True)
            attend = (lifted / total).astype(BF)
            log_totals.append(peak + jnp.log(total))
            attended_parts.append(
                jnp.einsum("hdk,hkq->hdq", values[:, :, :stop], attend, preferred_element_type=F32)
            )
        attended = (
            jnp.concatenate(attended_parts, axis=2).reshape(local_cols, seq_len).astype(BF)
        )
        attn_share = scatter4(mm(out_w, attended, ((0,), (0,))))
        residual_own = tokens_own.astype(F32) + attn_share + own_slice(out_bias)
        residual = gather4(residual_own.astype(BF)).astype(F32)
        mean_two, inv_two = norm_parts(residual)
        unit_two = (residual - mean_two) * inv_two
        unit_two_own = (residual_own - mean_two) * inv_two
        normed_two = (unit_two * gain_two[:, None] + shift_two[:, None]).astype(BF)

        pre_gelu = mm(up_w, normed_two, ((0,), (0,))) + up_b
        active, gelu_pull = jax.vjp(lambda inner: jax.nn.gelu(inner, approximate=True), pre_gelu)
        active_low = active.astype(BF)
        grad_active = mm(down_w, cot, ((1,), (0,)))
        grad_pre = gelu_pull(grad_active)[0].astype(BF)
        grad_normed_part = mm(up_w, grad_pre, ((1,), (0,)))
        scaled_part = grad_normed_part * gain_two[:, None]
        sums_two = sums4(
            jnp.concatenate(
                [
                    jnp.sum(scaled_part, axis=0, keepdims=True),
                    jnp.sum(scaled_part * unit_two, axis=0, keepdims=True),
                ],
                axis=0,
            )
        )
        grad_normed_two = scatter4(grad_normed_part)

        down_share = scatter4(mm(down_w, active_low, ((0,), (0,))))
        output = (residual_own + down_share + own_slice(down_bias)).astype(BF)
        output = send(output, regroup)

        down_grad = mm(active_low, cot, ((1,), (1,)))
        up_grad = mm(normed_two, grad_pre, ((1,), (1,)))

        cot_own32 = cot_own.astype(F32)
        grad_residual = (
            inv_two
            * (
                grad_normed_two * own_slice(gain_two)
                - sums_two[0:1] / model
                - unit_two_own * (sums_two[1:2] / model)
            )
            + cot_own32
        )
        grad_branch = gather4(grad_residual.astype(BF))
        out_grad = mm(attended, grad_branch, ((1,), (1,)))
        grad_attended = (
            mm(out_w, grad_branch, ((1,), (0,))).astype(BF).reshape(head_count, HD, seq_len)
        )

        query_parts = []
        key_grad = jnp.zeros((head_count, HD, seq_len), F32)
        value_grad = jnp.zeros((head_count, HD, seq_len), F32)
        for block in range(block_count):
            start, stop = block * block_rows, (block + 1) * block_rows
            attend_full = jnp.exp(scores_of(start, stop) - log_totals[block])
            attend = attend_full.astype(BF)
            grad_here = grad_attended[:, :, start:stop]
            grad_attend = jnp.einsum(
                "hdk,hdq->hkq", values[:, :, :stop], grad_here, preferred_element_type=F32
            )
            grad_scores = (
                attend_full
                * (grad_attend - jnp.sum(attend_full * grad_attend, axis=1, keepdims=True))
            ).astype(BF)
            query_parts.append(
                jnp.einsum(
                    "hdk,hkq->hdq", keys[:, :, :stop], grad_scores, preferred_element_type=F32
                )
                * score_scale
            )
            key_grad = key_grad.at[:, :, :stop].add(
                jnp.einsum(
                    "hdq,hkq->hdk",
                    queries[:, :, start:stop],
                    grad_scores,
                    preferred_element_type=F32,
                )
                * score_scale
            )
            value_grad = value_grad.at[:, :, :stop].add(
                jnp.einsum("hdq,hkq->hdk", grad_here, attend, preferred_element_type=F32)
            )
        grad_proj = (
            jnp.concatenate([jnp.concatenate(query_parts, axis=2), key_grad, value_grad], axis=0)
            .reshape(3 * local_cols, seq_len)
            .astype(BF)
        )
        grad_one_part = mm(qkv_t, grad_proj, ((0,), (0,)))
        scaled_one = grad_one_part * gain_one[:, None]
        sums_one = sums4(
            jnp.concatenate(
                [
                    jnp.sum(scaled_one, axis=0, keepdims=True),
                    jnp.sum(scaled_one * unit_one, axis=0, keepdims=True),
                ],
                axis=0,
            )
        )
        grad_normed_one = scatter4(grad_one_part)
        qkv_grad = mm(grad_proj, normed_low, ((1,), (1,)))
        unit_one_own = (tokens_own.astype(F32) - mean_one) * inv_one
        grad_tokens = (
            inv_one
            * (
                grad_normed_one * own_slice(gain_one)
                - sums_one[0:1] / model
                - unit_one_own * (sums_one[1:2] / model)
            )
            + grad_residual
        ).astype(BF)
        grad_tokens = send(grad_tokens, regroup)

        def reduce_parts(grad, first):
            order = ((b0, swap_b0, home_b0), (b1, swap_b1, home_b1))
            if first:
                order = order[::-1]
            value = grad
            rows = []
            for bit, pairs, _ in order:
                rows.append(value.shape[0])
                keep, away = split(value, bit)
                value = keep + send(away.astype(BF), pairs).astype(F32)
            if high > 1:
                value = lax.psum(value, "hi")
            value = (value + send(value.astype(BF), home_send).astype(F32)).astype(BF)
            for (bit, _, pairs), count in zip(order[::-1], rows[::-1]):
                value = merge(value, send(value, pairs), bit, count)
            return jnp.where(home, value, send(value, home_core)).astype(F32)

        up_sum = reduce_parts(up_grad, 0)
        down_sum = reduce_parts(down_grad, 1)
        out_sum = reduce_parts(out_grad, 0)
        qkv_rows = qkv_grad.shape[0]
        cut = half_rows(qkv_rows)
        qkv_sum = jnp.concatenate(
            [
                reduce_parts(qkv_grad[:cut], 0)[: qkv_rows - cut],
                reduce_parts(qkv_grad[qkv_rows - cut :], 1),
            ],
            axis=0,
        )

        proj32 = grad_proj.astype(F32)
        small = jnp.concatenate(
            [
                jnp.sum(proj32[:local_cols], axis=1),
                jnp.sum(proj32[2 * local_cols :], axis=1),
                jnp.sum(grad_residual, axis=1),
                jnp.sum(grad_normed_one * unit_one_own, axis=1),
                jnp.sum(grad_normed_one, axis=1),
                jnp.sum(grad_normed_two * unit_two_own, axis=1),
                jnp.sum(grad_normed_two, axis=1),
                jnp.sum(cot_own32, axis=1),
                jnp.sum(grad_pre.astype(F32), axis=1),
            ]
        )
        small = small + send(small, swap_b0)
        small = small + send(small, swap_b1)
        if high > 1:
            small = lax.psum(small, "hi")
        small = small + send(small, swap_high)
        small = jnp.where(home, small, send(small, swap_core))
        pieces = [small[i * share : (i + 1) * share] for i in range(8)]
        return (
            output.T,
            grad_tokens.T,
            qkv_sum.reshape(3, local_cols, model).transpose(2, 0, 1),
            small[: 2 * local_cols].reshape(2, local_cols),
            out_sum,
            pieces[2],
            pieces[3],
            pieces[4],
            pieces[5],
            pieces[6],
            up_sum,
            small[8 * share :],
            down_sum,
            pieces[7],
        )

    return per_device


def solution(mesh):
    high = mesh.shape["wide"] // 8
    grid = Mesh(mesh.devices.reshape(high, 2, 2, 2, 2, 2), AXES)
    wide = ("hi", "b1", "b0", "core")
    narrow = ("zh", "zl")
    return jax.shard_map(
        build(high),
        mesh=grid,
        in_specs=(
            P(wide, narrow),
            P(wide),
            P(None, None, narrow),
            P(None, narrow),
            P(narrow, None),
            P(),
            P(),
            P(),
            P(),
            P(),
            P(None, narrow),
            P(narrow),
            P(narrow, None),
            P(),
            P(wide, narrow),
        ),
        out_specs=(
            P(wide, narrow),
            P(wide, narrow),
            P(None, None, narrow),
            P(None, narrow),
            P(narrow, None),
            P(narrow),
            P(narrow),
            P(narrow),
            P(narrow),
            P(narrow),
            P(None, narrow),
            P(narrow),
            P(narrow, None),
            P(narrow),
        ),
        check_vma=False,
    )
```
